32 devices in a mesh: row: 2 (over x), col: 16 (over z, y, core).
Axes of the slice: x: 2, y: 2, z: 4, core: 2. Of those that a mesh axis runs over, the one named last changes fastest.
Arguments:
- chol_window: bfloat16 [512, 8, 1024], P('row', None, 'col'), may hold values from -6 to 6
- pair_vectors: bfloat16 [512, 512, 1024], P('row', 'col'), may hold values from -0.1875 to 0.1875
- amplitudes: bfloat16 [512, 512, 256], P('row', 'col'), may hold values from -0.015625 to 0.015625
Outputs:
- ladder: float32 [8, 256, 512], P(None, 'col', 'row')
The draws below stay inside these ranges and needn't reach their ends.
All inputs are finite; a program needn't handle non-finite values.
Results may differ from the reference program's by a relative error of at most 0.0029.
Values may be sent and summed in bfloat16 or wider, within the bound.
A program may use at most 320 MiB of HBM per device.

```python
import jax
import jax.numpy as jnp
from jax import lax

V = 512
NQ = 1024
NA = 8
NP = 256


def strengthened(result, rng, source, target, shards_of, factor):
    def block_of(axis_at):
        return (jnp.arange(result.shape[axis_at]) // (result.shape[axis_at] // shards_of)).reshape((-1,) + (1,) * (result.ndim - 1 - axis_at))

    first = jax.random.permutation(rng, shards_of)[block_of(target)]
    second = (block_of(target) + shards_of // 2) % shards_of
    return jnp.where((block_of(source) == first) | (block_of(source) == second), factor * result, result)


def shard_levels(rng, dims, pieces, low, largest):
    def one(position, blocks):
        draws = jax.random.uniform(jax.random.fold_in(jax.random.fold_in(rng, 6), position), (blocks,), jnp.float32, low / len(pieces), largest / len(pieces))
        return jnp.repeat(jnp.exp(draws), dims[position] // blocks).reshape((-1,) + (1,) * (len(dims) - position - 1))

    level = one(*pieces[0])
    for cut in pieces[1:]:
        level = level * one(*cut)
    return level


def centred(key, shape, spread, bound, pieces=(), dtype=jnp.bfloat16):
    level = shard_levels(key, shape, pieces, -0.22, 0.18) if pieces else 1.0
    array = jax.random.normal(key, shape, jnp.float32) * spread * level
    return jnp.minimum(jnp.maximum(array, -bound), bound).astype(dtype)


def gaussian_with(key, dims, deviation, limit, shards, heavy, dtype=jnp.bfloat16):
    drawn = deviation * jax.random.normal(key, dims, jnp.float32)
    if shards:
        drawn = drawn * shard_levels(key, dims, shards, -0.22, 0.18)
    return jnp.clip(strengthened(drawn, jax.random.fold_in(key, 3), *heavy), -limit, limit).astype(dtype)


def setup_inputs(seed: int = 0) -> dict:
    key_of = jax.random.split(jax.random.key(seed), 4)
    chol_window = centred(key_of[0], (V, NA, NQ), 1.0, 6.0, ((0, 2), (2, 16)))
    pair_vectors = centred(key_of[1], (V, V, NQ), NQ ** -0.5, 0.1875, ((0, 2), (1, 16)))
    amplitudes = gaussian_with(key_of[2], (V, V, NP), (V * V) ** -0.5, 0.015625, ((0, 2), (1, 16)), (1, 2, 16, 2.0))
    return dict(chol_window=chol_window, pair_vectors=pair_vectors, amplitudes=amplitudes)


def reference(chol_window, pair_vectors, amplitudes):
    block_rows = 16
    flat_window = chol_window.reshape(V * NA, NQ)
    stacked = pair_vectors.reshape(V // block_rows, block_rows * V, NQ)
    amps_wide = amplitudes.astype(jnp.float32)

    def one_block(vectors):
        integrals = lax.dot_general(flat_window, vectors, (((1,), (1,)), ((), ())), preferred_element_type=jnp.float32)
        integrals = integrals.astype(jnp.bfloat16).astype(jnp.float32).reshape(V, NA, block_rows, V)
        return jnp.einsum("cabd,cdn->anb", integrals, amps_wide, precision=lax.Precision.HIGHEST)

    pieces_out = lax.map(one_block, stacked)
    return pieces_out.transpose(1, 2, 0, 3).reshape(NA, NP, V)
```

```python
import functools

import jax
import jax.numpy as jnp
from jax import lax
from jax.experimental import pallas as pl
from jax.experimental.pallas import tpu as pltpu
from jax.sharding import PartitionSpec as P

MESH = pl.DeviceIdType.MESH
D_BLOCK = 4
P_ROWS = 32
T_PAIR = 2
T_AHEAD = 3
T_EACH = 2


def ladder_kernel(c, last, first, p_ref, w_ref, t_ref, *rest):
    if first:
        out_ref, it, acc = rest
    else:
        prev_ref, out_ref, it, acc = rest
    step = pl.program_id(0)
    d_block, b, q = p_ref.shape
    groups = w_ref.shape[1] // c
    n = t_ref.shape[2]

    @pl.when(step == 0)
    def _():
        acc[...] = jnp.zeros_like(acc) if first else prev_ref[...]

    rows = p_ref[...].reshape(d_block * b, q)
    for a in range(groups):
        term = jnp.dot(rows, w_ref[:, a * c:(a + 1) * c], preferred_element_type=jnp.float32)
        term = term.astype(jnp.bfloat16)
        for d in range(d_block):
            it[a * b:(a + 1) * b, d * c:(d + 1) * c] = term[d * b:(d + 1) * b]
    acc[...] += jnp.dot(it[...], t_ref[...].reshape(d_block * c, n), preferred_element_type=jnp.float32)

    @pl.when(step == pl.num_programs(0) - 1)
    def _():
        out_ref[...] = acc[...].T if last else acc[...]


def ladder_call(p_t, w, t, prev, last):
    d, b, q = p_t.shape
    c, n = t.shape[1], t.shape[2]
    width = w.shape[1]
    rows = width // c * b
    d_block = D_BLOCK if d % D_BLOCK == 0 else 1
    out = (n, rows) if last else (rows, n)
    whole = lambda shape: pl.BlockSpec(shape, lambda i: (0,) * len(shape))
    in_specs = [
        pl.BlockSpec((d_block, b, q), lambda i: (i, 0, 0)),
        whole((q, width)),
        pl.BlockSpec((d_block, c, n), lambda i: (i, 0, 0)),
    ]
    args = [p_t, w, t]
    if prev is not None:
        in_specs.append(whole((rows, n)))
        args.append(prev)
    flops = 2 * d * b * width * (q + n)
    return pl.pallas_call(
        functools.partial(ladder_kernel, c, last, prev is None),
        out_shape=jax.ShapeDtypeStruct(out, jnp.float32),
        grid=(d // d_block,),
        in_specs=in_specs,
        out_specs=whole(out),
        scratch_shapes=[
            pltpu.VMEM((rows, d_block * c), jnp.bfloat16),
            pltpu.VMEM((rows, n), jnp.float32),
        ],
        cost_estimate=pl.CostEstimate(flops=flops, bytes_accessed=2 * (p_t.size + w.size + t.size), transcendentals=0),
        compiler_params=pltpu.CompilerParams(vmem_limit_bytes=60 * 2**20),
    )(*args)


def scatter_kernel(cols, pair, x_ref, out_ref, near, sums, far, near_send, near_recv, far_send, far_recv):
    me = lax.axis_index("col")
    pairs = cols // pair
    core, mine = lax.rem(me, pair), lax.div(me, pair)
    partner = mine * pair + lax.rem(core + 1, pair)

    def place(s):
        return lax.rem(mine + s, pairs) * pair

    barrier = pltpu.get_barrier_semaphore()
    others = [place(s) + core for s in range(1, pairs)] + [partner] * (pair - 1)
    for other in others:
        pl.semaphore_signal(barrier, inc=1, device_id={"col": other}, device_id_type=MESH)
    pl.semaphore_wait(barrier, len(others))

    order = [*range(1, pairs), 0]
    near_copies = {}
    if pair == 2:
        for s in order:
            near_copies[s] = pltpu.make_async_remote_copy(
                src_ref=x_ref.at[place(s) + lax.rem(core + 1, pair)],
                dst_ref=near.at[s],
                send_sem=near_send.at[s],
                recv_sem=near_recv.at[s],
                device_id={"col": partner},
                device_id_type=MESH,
            )
            near_copies[s].start()

    def pair_sum(s):
        own = x_ref[place(s) + core]
        if pair == 1:
            return own
        near_copies[s].wait_recv()
        return own + near[s]

    far_copies = []
    for s in range(1, pairs):
        sums[s - 1] = pair_sum(s).astype(sums.dtype)
        copy = pltpu.make_async_remote_copy(
            src_ref=sums.at[s - 1],
            dst_ref=far.at[s - 1],
            send_sem=far_send.at[s - 1],
            recv_sem=far_recv.at[s - 1],
            device_id={"col": place(s) + core},
            device_id_type=MESH,
        )
        copy.start()
        far_copies.append(copy)
    total = pair_sum(0)
    for s, copy in enumerate(far_copies):
        copy.wait_recv()
        total = total + far[s].astype(jnp.float32)
    out_ref[...] = total
    for copy in far_copies:
        copy.wait_send()
    for copy in near_copies.values():
        copy.wait_send()


def scatter_call(x, cols):
    n, width = x.shape
    piece = (n // cols, width)
    pair = 2 if cols % 2 == 0 else 1
    pairs = cols // pair
    far = max(pairs - 1, 1)
    return pl.pallas_call(
        functools.partial(scatter_kernel, cols, pair),
        out_shape=jax.ShapeDtypeStruct(piece, jnp.float32),
        in_specs=[pl.BlockSpec(memory_space=pltpu.VMEM)],
        out_specs=pl.BlockSpec(memory_space=pltpu.VMEM),
        scratch_shapes=[
            pltpu.VMEM((pairs, *piece), jnp.float32),
            pltpu.VMEM((far, *piece), jnp.bfloat16),
            pltpu.VMEM((far, *piece), jnp.bfloat16),
            pltpu.SemaphoreType.DMA((pairs,)),
            pltpu.SemaphoreType.DMA((pairs,)),
            pltpu.SemaphoreType.DMA((far,)),
            pltpu.SemaphoreType.DMA((far,)),
        ],
        compiler_params=pltpu.CompilerParams(collective_id=0, has_side_effects=True),
    )(x.reshape(cols, *piece))


GROUP = 16


def routes(cols):
    return cols // 4, 2, 2


def fused_kernel(cols, w_in, p_in, t_in, out_ref, pt, p_raw, w, tt, t_raw, it, it_far, acc,
                 p_sem, t_sem, own_sem, xw_send, xw_recv, xt_send, xt_recv,
                 z_send, z_recv, y_send, y_recv, core_send, core_recv):
    d, b, q = pt.shape
    widths = w_in.shape[0]
    c, n = tt.shape[2], tt.shape[3]
    zs, _, _ = routes(cols)
    row, me = lax.axis_index("row"), lax.axis_index("col")
    core, y, z = lax.rem(me, 2), lax.rem(lax.div(me, 2), 2), lax.div(me, 4)
    slabs = 2 * widths
    p_rows = p_raw.shape[1]
    p_parts = b // p_rows
    t_pair = d // xt_send.shape[0]

    def col(z, y, core):
        return {"col": (z * 2 + y) * 2 + core}

    def p_copy(i):
        slot = lax.rem(i, 2)
        return pltpu.make_async_copy(p_in.at[pl.ds(i * p_rows, p_rows)], p_raw.at[slot], p_sem.at[slot])

    t_copy = pltpu.make_async_copy(t_in, t_raw, t_sem)
    own_copy = pltpu.make_async_copy(w_in, w.at[0, :, z, y, core], own_sem)
    own_copy.start()
    t_copy.start()
    p_copy(0).start()
    p_copy(1).start()

    barrier = pltpu.get_barrier_semaphore()
    others = [col(lax.rem(z + s, zs), y, core) for s in range(1, zs)]
    others += [col(z, 1 - y, core), col(z, y, 1 - core), {"row": 1 - row}]
    for other in others:
        pl.semaphore_signal(barrier, inc=1, device_id=other, device_id_type=MESH)
    pl.semaphore_wait(barrier, len(others))

    def remote(src, dst, send, recv, device):
        return pltpu.make_async_remote_copy(
            src_ref=src, dst_ref=dst, send_sem=send, recv_sem=recv, device_id=device, device_id_type=MESH)

    def place(g):
        return lax.div(g, widths), lax.rem(g, widths)

    def z_copy(g, s):
        h, a = place(g)
        piece = w.at[h, a, z, y, core]
        return remote(piece, piece, z_send.at[g, s - 1], z_recv.at[g, s - 1], col(lax.rem(z + s, zs), y, core))

    def y_copy(g):
        h, a = place(g)
        piece = w.at[h, a, :, y, core]
        return remote(piece, piece, y_send.at[g], y_recv.at[g], col(z, 1 - y, core))

    def core_copy(g):
        h, a = place(g)
        piece = w.at[h, a, :, :, core]
        return remote(piece, piece, core_send.at[g], core_recv.at[g], col(z, y, 1 - core))

    def t_far(i):
        piece = pl.ds(i * t_pair, t_pair)
        return remote(tt.at[0, piece], tt.at[1, piece], xt_send.at[i], xt_recv.at[i], {"row": 1 - row})

    w_far = remote(w_in, w.at[1, :, z, y, core], xw_send, xw_recv, {"row": 1 - row})

    def send_z(g):
        for s in range(1, zs):
            z_copy(g, s).start()

    def send_y(g):
        for s in range(1, zs):
            z_copy(g, s).wait_recv()
        y_copy(g).start()

    def send_core(g):
        y_copy(g).wait_recv()
        core_copy(g).start()

    w_far.start()
    own_copy.wait()
    send_z(0)
    send_z(1)

    index = lax.broadcasted_iota(jnp.int32, (GROUP * GROUP, GROUP * GROUP), 0)
    source = lax.broadcasted_iota(jnp.int32, (GROUP * GROUP, GROUP * GROUP), 1)
    swap = (lax.rem(index, GROUP) * GROUP + lax.div(index, GROUP) == source).astype(jnp.bfloat16)

    def swapped(block):
        width = block.shape[2]
        moved = jnp.dot(swap, block.reshape(GROUP * GROUP, width), preferred_element_type=jnp.float32)
        return moved.astype(jnp.bfloat16).reshape(GROUP, GROUP, width)

    t_copy.wait()
    for j in range(0, d, GROUP):
        for i in range(0, c, GROUP):
            tt[0, j:j + GROUP, i:i + GROUP] = swapped(t_raw[i:i + GROUP, j:j + GROUP])
        if j == 0:
            for i in range(T_AHEAD):
                t_far(i).start()

    def arrange(i, carry):
        p_copy(i).wait()
        slot = lax.rem(i, 2)
        for r in range(0, p_rows, GROUP):
            for j in range(0, d, GROUP):
                rows = pl.ds(pl.multiple_of(i * p_rows + r, GROUP), GROUP)
                pt[j:j + GROUP, rows] = swapped(p_raw[slot, r:r + GROUP, j:j + GROUP])

        @pl.when(i + 2 < p_parts)
        def _():
            p_copy(i + 2).start()

        return carry

    cut1, cut2 = p_parts // 3, 2 * p_parts // 3
    lax.fori_loop(0, cut1, arrange, 0)
    send_y(0)
    send_z(2)
    lax.fori_loop(cut1, cut2, arrange, 0)
    send_core(0)
    send_y(1)
    send_z(3)
    lax.fori_loop(cut2, p_parts, arrange, 0)
    w_far.wait_recv()

    def integrals(h, a, j, block):
        rows = pt[j:j + block].reshape(block * b, q) if isinstance(j, int) else pt[pl.ds(j, block)].reshape(block * b, q)
        term = jnp.dot(rows, w[h, a].reshape(q, c), preferred_element_type=jnp.float32)
        return term.astype(jnp.bfloat16)

    half = d // 2

    def own(a, carry):
        @pl.when(a < 2)
        def _():
            send_core(a + 1)
            send_y(a + 2)
            send_z(a + 4)

        @pl.when(a >= 2)
        def _():
            @pl.when(a == 2)
            def _():
                send_core(3)

            @pl.when(a > 2)
            def _():
                send_core(2 * a - 2)
                send_core(2 * a - 1)

            send_y(2 * a)
            send_y(2 * a + 1)

            @pl.when(a < widths - 1)
            def _():
                send_z(2 * a + 2)
                send_z(2 * a + 3)

        for i in range(T_EACH):
            i = T_AHEAD + T_EACH * a + i

            @pl.when(i < xt_send.shape[0])
            def _():
                t_far(i).start()

        core_copy(a).wait_recv()
        for j in range(0, d, D_BLOCK):
            term = integrals(0, a, j, D_BLOCK)
            for e in range(D_BLOCK):
                it[:, (j + e) * c:(j + e + 1) * c] = term[e * b:(e + 1) * b]
        acc[pl.ds(a * b, b)] = jnp.dot(it[...], tt[0].reshape(d * c, n), preferred_element_type=jnp.float32)
        return carry

    lax.fori_loop(0, widths, own, 0)
    send_core(slabs - 2)
    send_core(slabs - 1)
    for i in range(half // t_pair):
        t_far(i).wait_recv()

    def far(a, carry):
        core_copy(widths + a).wait_recv()
        for j in range(0, half, D_BLOCK):
            term = integrals(1, a, j, D_BLOCK)
            for e in range(D_BLOCK):
                it[:, (j + e) * c:(j + e + 1) * c] = term[e * b:(e + 1) * b]
        acc[pl.ds(a * b, b)] += jnp.dot(
            it[:, :half * c], tt[1, :half].reshape(half * c, n), preferred_element_type=jnp.float32)
        return carry

    lax.fori_loop(0, widths, far, 0)

    def late(i, carry):
        j = half + i * D_BLOCK
        for a in range(widths):
            term = integrals(1, a, j, D_BLOCK)
            for e in range(D_BLOCK):
                it_far[a * b:(a + 1) * b, e * c:(e + 1) * c] = term[e * b:(e + 1) * b]
        for s in range(D_BLOCK // t_pair):
            t_far(lax.div(j, t_pair) + s).wait_recv()
        acc[...] += jnp.dot(
            it_far[...], tt[1, pl.ds(j, D_BLOCK)].reshape(D_BLOCK * c, n), preferred_element_type=jnp.float32)
        return carry

    lax.fori_loop(0, half // D_BLOCK, late, 0)
    out_ref[...] = acc[...].T

    def drain(g, carry):
        for s in range(1, zs):
            z_copy(g, s).wait_send()
        y_copy(g).wait_send()
        core_copy(g).wait_send()
        return carry

    lax.fori_loop(0, slabs, drain, 0)

    def drain_t(i, carry):
        t_far(i).wait_send()
        return carry

    lax.fori_loop(0, xt_send.shape[0], drain_t, 0)
    w_far.wait_send()


def fused_call(cols, chol_window, pair_vectors, amplitudes):
    c, widths, q_own = chol_window.shape
    b, d, q = pair_vectors.shape
    n = amplitudes.shape[2]
    zs, ys, cores = routes(cols)
    slabs = 2 * widths
    sends = d // T_PAIR
    rows = widths * b
    dma = pltpu.SemaphoreType.DMA
    hbm = pl.BlockSpec(memory_space=pl.ANY)
    return pl.pallas_call(
        functools.partial(fused_kernel, cols),
        out_shape=jax.ShapeDtypeStruct((n, rows), jnp.float32),
        in_specs=[hbm, hbm, hbm],
        out_specs=pl.BlockSpec(memory_space=pltpu.VMEM),
        scratch_shapes=[
            pltpu.VMEM((d, b, q), jnp.bfloat16),
            pltpu.VMEM((2, P_ROWS, d, q), jnp.bfloat16),
            pltpu.VMEM((2, widths, zs, ys, cores, q_own, c), jnp.bfloat16),
            pltpu.VMEM((2, d, c, n), jnp.bfloat16),
            pltpu.VMEM((c, d, n), jnp.bfloat16),
            pltpu.VMEM((b, d * c), jnp.bfloat16),
            pltpu.VMEM((rows, D_BLOCK * c), jnp.bfloat16),
            pltpu.VMEM((rows, n), jnp.float32),
            dma((2,)), dma, dma, dma, dma, dma((sends,)), dma((sends,)),
            dma((slabs, zs - 1)), dma((slabs, zs - 1)),
            dma((slabs,)), dma((slabs,)), dma((slabs,)), dma((slabs,)),
        ],
        cost_estimate=pl.CostEstimate(
            flops=2 * d * b * 2 * c * widths * (q + n), bytes_accessed=2 * (b * d * q + c * d * n), transcendentals=0),
        compiler_params=pltpu.CompilerParams(collective_id=1, has_side_effects=True, vmem_limit_bytes=60 * 2**20),
    )(chol_window.transpose(1, 2, 0), pair_vectors, amplitudes)


def fits(rows, cols, chol_window, pair_vectors, amplitudes):
    c, widths, q_own = chol_window.shape
    b, d, q = pair_vectors.shape
    n = amplitudes.shape[2]
    held = 2 * (d * b * q + 2 * P_ROWS * d * q + 2 * widths * q * c + 3 * d * c * n + b * d * c + widths * b * D_BLOCK * c)
    held += 8 * widths * b * n
    return (rows == 2 and cols % 4 == 0 and cols > 4 and widths >= 4 and c % 128 == 0 and n % 128 == 0 and q % 128 == 0
            and b % P_ROWS == 0 and b // P_ROWS >= 3 and d % (2 * GROUP) == 0 and q_own % GROUP == 0
            and held <= 56 * 2**20)


def local(row_count, col_count, chol_window, pair_vectors, amplitudes):
    c, width_a, q_own = chol_window.shape
    b = pair_vectors.shape[0]

    if fits(row_count, col_count, chol_window, pair_vectors, amplitudes):
        total = fused_call(col_count, chol_window, pair_vectors, amplitudes)
        out = scatter_call(total, col_count)
        return out.reshape(out.shape[0], width_a, b).transpose(1, 0, 2)

    w_own = chol_window.transpose(2, 1, 0)
    t_own = amplitudes.transpose(1, 0, 2)
    if row_count == 1:
        blocks = [(w_own, t_own)]
    elif c % 128 == 0:
        blocks = [(w_own, t_own)]
        for shift in range(1, row_count):
            pairs = [(i, (i + shift) % row_count) for i in range(row_count)]
            w_far, t_held = lax.optimization_barrier((lax.ppermute(w_own, "row", pairs), t_own))
            blocks.append((w_far, lax.ppermute(t_held, "row", pairs)))
    else:
        blocks = [(
            lax.all_gather(w_own, "row", axis=2, tiled=True),
            lax.all_gather(t_own, "row", axis=1, tiled=True),
        )]
    p_t = pair_vectors.transpose(1, 0, 2)

    total = None
    for index, (w, t) in enumerate(blocks):
        w = lax.all_gather(w.reshape(q_own, -1), "col", axis=0, tiled=True)
        total = ladder_call(p_t, w, t, total, index == len(blocks) - 1)
    out = scatter_call(total, col_count)
    return out.reshape(out.shape[0], width_a, b).transpose(1, 0, 2)


def solution(mesh):
    return jax.shard_map(
        functools.partial(local, mesh.shape["row"], mesh.shape["col"]),
        mesh=mesh,
        in_specs=(P("row", None, "col"), P("row", "col", None), P("row", "col", None)),
        out_specs=P(None, "col", "row"),
        check_vma=False,
    )
```

```python
import functools

import jax
import jax.numpy as jnp
from jax import lax
from jax.experimental import pallas as pl
from jax.experimental.pallas import tpu as pltpu
from jax.sharding import PartitionSpec as P

MESH = pl.DeviceIdType.MESH
D_BLOCK = 4
P_ROWS = 32
T_PAIR = 2
T_AHEAD = 4
T_EACH = 2
SPANS = (0.25, 0.5, 0.75, 0.875)
LAST = 8


def ladder_kernel(c, last, first, p_ref, w_ref, t_ref, *rest):
    if first:
        out_ref, it, acc = rest
    else:
        prev_ref, out_ref, it, acc = rest
    step = pl.program_id(0)
    d_block, b, q = p_ref.shape
    groups = w_ref.shape[1] // c
    n = t_ref.shape[2]

    @pl.when(step == 0)
    def _():
        acc[...] = jnp.zeros_like(acc) if first else prev_ref[...]

    rows = p_ref[...].reshape(d_block * b, q)
    for a in range(groups):
        term = jnp.dot(rows, w_ref[:, a * c:(a + 1) * c], preferred_element_type=jnp.float32)
        term = term.astype(jnp.bfloat16)
        for d in range(d_block):
            it[a * b:(a + 1) * b, d * c:(d + 1) * c] = term[d * b:(d + 1) * b]
    acc[...] += jnp.dot(it[...], t_ref[...].reshape(d_block * c, n), preferred_element_type=jnp.float32)

    @pl.when(step == pl.num_programs(0) - 1)
    def _():
        out_ref[...] = acc[...].T if last else acc[...]


def ladder_call(p_t, w, t, prev, last):
    d, b, q = p_t.shape
    c, n = t.shape[1], t.shape[2]
    width = w.shape[1]
    rows = width // c * b
    d_block = D_BLOCK if d % D_BLOCK == 0 else 1
    out = (n, rows) if last else (rows, n)
    whole = lambda shape: pl.BlockSpec(shape, lambda i: (0,) * len(shape))
    in_specs = [
        pl.BlockSpec((d_block, b, q), lambda i: (i, 0, 0)),
        whole((q, width)),
        pl.BlockSpec((d_block, c, n), lambda i: (i, 0, 0)),
    ]
    args = [p_t, w, t]
    if prev is not None:
        in_specs.append(whole((rows, n)))
        args.append(prev)
    flops = 2 * d * b * width * (q + n)
    return pl.pallas_call(
        functools.partial(ladder_kernel, c, last, prev is None),
        out_shape=jax.ShapeDtypeStruct(out, jnp.float32),
        grid=(d // d_block,),
        in_specs=in_specs,
        out_specs=whole(out),
        scratch_shapes=[
            pltpu.VMEM((rows, d_block * c), jnp.bfloat16),
            pltpu.VMEM((rows, n), jnp.float32),
        ],
        cost_estimate=pl.CostEstimate(flops=flops, bytes_accessed=2 * (p_t.size + w.size + t.size), transcendentals=0),
        compiler_params=pltpu.CompilerParams(vmem_limit_bytes=60 * 2**20),
    )(*args)


def scatter_kernel(cols, pair, x_ref, out_ref, near, sums, far, near_send, near_recv, far_send, far_recv):
    me = lax.axis_index("col")
    pairs = cols // pair
    core, mine = lax.rem(me, pair), lax.div(me, pair)
    partner = mine * pair + lax.rem(core + 1, pair)

    def place(s):
        return lax.rem(mine + s, pairs) * pair

    barrier = pltpu.get_barrier_semaphore()
    others = [place(s) + core for s in range(1, pairs)] + [partner] * (pair - 1)
    for other in others:
        pl.semaphore_signal(barrier, inc=1, device_id={"col": other}, device_id_type=MESH)
    pl.semaphore_wait(barrier, len(others))

    order = [*range(1, pairs), 0]
    near_copies = {}
    if pair == 2:
        for s in order:
            near_copies[s] = pltpu.make_async_remote_copy(
                src_ref=x_ref.at[place(s) + lax.rem(core + 1, pair)],
                dst_ref=near.at[s],
                send_sem=near_send.at[s],
                recv_sem=near_recv.at[s],
                device_id={"col": partner},
                device_id_type=MESH,
            )
            near_copies[s].start()

    def pair_sum(s):
        own = x_ref[place(s) + core]
        if pair == 1:
            return own
        near_copies[s].wait_recv()
        return own + near[s]

    far_copies = []
    for s in range(1, pairs):
        sums[s - 1] = pair_sum(s).astype(sums.dtype)
        copy = pltpu.make_async_remote_copy(
            src_ref=sums.at[s - 1],
            dst_ref=far.at[s - 1],
            send_sem=far_send.at[s - 1],
            recv_sem=far_recv.at[s - 1],
            device_id={"col": place(s) + core},
            device_id_type=MESH,
        )
        copy.start()
        far_copies.append(copy)
    total = pair_sum(0)
    for s, copy in enumerate(far_copies):
        copy.wait_recv()
        total = total + far[s].astype(jnp.float32)
    out_ref[...] = total
    for copy in far_copies:
        copy.wait_send()
    for copy in near_copies.values():
        copy.wait_send()


def scatter_call(x, cols):
    n, width = x.shape
    piece = (n // cols, width)
    pair = 2 if cols % 2 == 0 else 1
    pairs = cols // pair
    far = max(pairs - 1, 1)
    return pl.pallas_call(
        functools.partial(scatter_kernel, cols, pair),
        out_shape=jax.ShapeDtypeStruct(piece, jnp.float32),
        in_specs=[pl.BlockSpec(memory_space=pltpu.VMEM)],
        out_specs=pl.BlockSpec(memory_space=pltpu.VMEM),
        scratch_shapes=[
            pltpu.VMEM((pairs, *piece), jnp.float32),
            pltpu.VMEM((far, *piece), jnp.bfloat16),
            pltpu.VMEM((far, *piece), jnp.bfloat16),
            pltpu.SemaphoreType.DMA((pairs,)),
            pltpu.SemaphoreType.DMA((pairs,)),
            pltpu.SemaphoreType.DMA((far,)),
            pltpu.SemaphoreType.DMA((far,)),
        ],
        compiler_params=pltpu.CompilerParams(collective_id=0, has_side_effects=True),
    )(x.reshape(cols, *piece))


GROUP = 16


def routes(cols):
    return cols // 4, 2, 2


def fused_kernel(cols, spans, w_in, p_in, t_in, out_ref, pt, p_raw, w, tt, t_raw, it, it_far, acc,
                 x, near, far_out, far_in,
                 p_sem, t_sem, own_sem, xw_send, xw_recv, xt_send, xt_recv,
                 z_send, z_recv, y_send, y_recv, core_send, core_recv,
                 near_send, near_recv, far_send, far_recv):
    d, b, q = pt.shape
    widths = w_in.shape[0]
    c, n = tt.shape[2], tt.shape[3]
    zs, _, _ = routes(cols)
    row, me = lax.axis_index("row"), lax.axis_index("col")
    core, y, z = lax.rem(me, 2), lax.rem(lax.div(me, 2), 2), lax.div(me, 4)
    slabs = 2 * widths
    p_rows = p_raw.shape[1]
    p_parts = b // p_rows
    t_pair = d // xt_send.shape[0]

    def col(z, y, core):
        return {"col": (z * 2 + y) * 2 + core}

    def p_copy(i):
        slot = lax.rem(i, 2)
        return pltpu.make_async_copy(p_in.at[pl.ds(i * p_rows, p_rows)], p_raw.at[slot], p_sem.at[slot])

    t_copy = pltpu.make_async_copy(t_in, t_raw, t_sem)
    own_copy = pltpu.make_async_copy(w_in, w.at[0, :, z, y, core], own_sem)
    own_copy.start()
    t_copy.start()
    p_copy(0).start()
    p_copy(1).start()

    barrier = pltpu.get_barrier_semaphore()
    others = [col(lax.rem(z + s, zs), y, core) for s in range(1, zs)]
    others += [col(lax.rem(z + s, zs), 1 - y, core) for s in range(zs)]
    others += [col(z, y, 1 - core), {"row": 1 - row}]
    for other in others:
        pl.semaphore_signal(barrier, inc=1, device_id=other, device_id_type=MESH)
    pl.semaphore_wait(barrier, len(others))

    def remote(src, dst, send, recv, device):
        return pltpu.make_async_remote_copy(
            src_ref=src, dst_ref=dst, send_sem=send, recv_sem=recv, device_id=device, device_id_type=MESH)

    def place(g):
        return lax.div(g, widths), lax.rem(g, widths)

    def z_copy(g, s):
        h, a = place(g)
        piece = w.at[h, a, z, y, core]
        return remote(piece, piece, z_send.at[g, s - 1], z_recv.at[g, s - 1], col(lax.rem(z + s, zs), y, core))

    def y_copy(g):
        h, a = place(g)
        piece = w.at[h, a, :, y, core]
        return remote(piece, piece, y_send.at[g], y_recv.at[g], col(z, 1 - y, core))

    def core_copy(g):
        h, a = place(g)
        piece = w.at[h, a, :, :, core]
        return remote(piece, piece, core_send.at[g], core_recv.at[g], col(z, y, 1 - core))

    def t_far(i):
        piece = pl.ds(i * t_pair, t_pair)
        return remote(tt.at[0, piece], tt.at[1, piece], xt_send.at[i], xt_recv.at[i], {"row": 1 - row})

    w_far = remote(w_in, w.at[1, :, z, y, core], xw_send, xw_recv, {"row": 1 - row})

    def send_z(g):
        for s in range(1, zs):
            z_copy(g, s).start()

    def send_y(g):
        for s in range(1, zs):
            z_copy(g, s).wait_recv()
        y_copy(g).start()

    def send_core(g):
        y_copy(g).wait_recv()
        core_copy(g).start()

    w_far.start()
    own_copy.wait()
    send_z(0)
    send_z(1)

    index = lax.broadcasted_iota(jnp.int32, (GROUP * GROUP, GROUP * GROUP), 0)
    source = lax.broadcasted_iota(jnp.int32, (GROUP * GROUP, GROUP * GROUP), 1)
    swap = (lax.rem(index, GROUP) * GROUP + lax.div(index, GROUP) == source).astype(jnp.bfloat16)

    def swapped(block):
        width = block.shape[2]
        moved = jnp.dot(swap, block.reshape(GROUP * GROUP, width), preferred_element_type=jnp.float32)
        return moved.astype(jnp.bfloat16).reshape(GROUP, GROUP, width)

    t_copy.wait()
    for j in range(0, d, GROUP):
        for i in range(0, c, GROUP):
            tt[0, j:j + GROUP, i:i + GROUP] = swapped(t_raw[i:i + GROUP, j:j + GROUP])
        if j == 0:
            for i in range(T_AHEAD):
                t_far(i).start()

    def arrange(i, carry):
        p_copy(i).wait()
        slot = lax.rem(i, 2)
        for r in range(0, p_rows, GROUP):
            for j in range(0, d, GROUP):
                rows = pl.ds(pl.multiple_of(i * p_rows + r, GROUP), GROUP)
                pt[j:j + GROUP, rows] = swapped(p_raw[slot, r:r + GROUP, j:j + GROUP])

        @pl.when(i + 2 < p_parts)
        def _():
            p_copy(i + 2).start()

        return carry

    cut1, cut2 = p_parts // 2 - 1, p_parts - 1
    lax.fori_loop(0, cut1, arrange, 0)
    send_y(0)
    send_z(2)
    lax.fori_loop(cut1, cut2, arrange, 0)
    send_y(1)
    send_z(3)
    lax.fori_loop(cut2, p_parts, arrange, 0)
    send_core(0)
    send_y(2)
    send_z(4)
    w_far.wait_recv()

    def integrals(h, a, j, block):
        rows = pt[j:j + block].reshape(block * b, q) if isinstance(j, int) else pt[pl.ds(j, block)].reshape(block * b, q)
        term = jnp.dot(rows, w[h, a].reshape(q, c), preferred_element_type=jnp.float32)
        return term.astype(jnp.bfloat16)

    half = d // 2

    def each(first, last, send):
        def body(g, carry):
            send(g)
            return carry

        lax.fori_loop(first + 1, jnp.minimum(last, slabs - 1) + 1, body, 0)

    def held(step):
        return jnp.maximum(2 * step - 1, step + 1)

    def passed(step):
        return jnp.maximum(2 * step + 2, 3)

    def advance(step):
        each(held(step - 1), held(step), send_core)
        each(passed(step - 1), passed(step), send_y)
        each(2 * step + 3, 2 * step + 5, send_z)

    def own_part(a, first, last):
        for j in range(first, last, D_BLOCK):
            term = integrals(0, a, j, D_BLOCK)
            for e in range(D_BLOCK):
                it[:, (j + e) * c:(j + e + 1) * c] = term[e * b:(e + 1) * b]

    def own_end(a):
        acc[pl.ds(a * b, b)] = jnp.dot(it[...], tt[0].reshape(d * c, n), preferred_element_type=jnp.float32)

    core_copy(0).wait_recv()
    own_part(0, 0, half)
    send_core(1)
    send_y(3)
    send_z(5)
    own_part(0, half, d)
    own_end(0)

    def own(a, carry):
        advance(a)
        for i in range(T_EACH):
            i = T_AHEAD + T_EACH * (a - 1) + i

            @pl.when(i < xt_send.shape[0])
            def _():
                t_far(i).start()

        core_copy(a).wait_recv()
        own_part(a, 0, d)
        own_end(a)
        return carry

    lax.fori_loop(1, widths, own, 0)
    for i in range(half // t_pair):
        t_far(i).wait_recv()

    def far(a, carry):
        advance(widths + a)
        core_copy(widths + a).wait_recv()
        for j in range(0, half, D_BLOCK):
            term = integrals(1, a, j, D_BLOCK)
            for e in range(D_BLOCK):
                it[:, (j + e) * c:(j + e + 1) * c] = term[e * b:(e + 1) * b]
        acc[pl.ds(a * b, b)] += jnp.dot(
            it[:, :half * c], tt[1, :half].reshape(half * c, n), preferred_element_type=jnp.float32)
        return carry

    lax.fori_loop(0, widths, far, 0)

    def late(i, carry):
        j = half + i * D_BLOCK
        for a in range(widths):
            term = integrals(1, a, j, D_BLOCK)
            for e in range(D_BLOCK):
                it_far[a * b:(a + 1) * b, e * c:(e + 1) * c] = term[e * b:(e + 1) * b]
        for s in range(D_BLOCK // t_pair):
            t_far(lax.div(j, t_pair) + s).wait_recv()
        acc[...] += jnp.dot(
            it_far[...], tt[1, pl.ds(j, D_BLOCK)].reshape(D_BLOCK * c, n), preferred_element_type=jnp.float32)
        return carry

    lax.fori_loop(0, half // D_BLOCK - LAST // D_BLOCK, late, 0)

    def near_copy(k):
        a = slice(*spans[k])
        return remote(x.at[a, :, :, 1 - core], near.at[a], near_send.at[k], near_recv.at[k], col(z, y, 1 - core))

    targets = [(s, side) for s in range(zs) for side in range(2)][1:]

    def place_of(m):
        s, side = targets[m]
        return lax.rem(z + s, zs), lax.rem(y + side, 2)

    def far_copy(k, m):
        a = slice(*spans[k])
        to = place_of(m)
        return remote(far_out.at[m, a], far_in.at[m, a], far_send.at[k, m], far_recv.at[k, m], col(*to, core))

    def slot(a, e=0, count=LAST):
        first = (a % (d // LAST)) * LAST + e
        return slice(first * c, (first + count) * c)

    def finish(k):
        for a in range(*spans[k]):
            r = slice(a * b, (a + 1) * b)
            last_t = tt[1, d - LAST:].reshape(LAST * c, n)
            whole = acc[r] + jnp.dot(it[:, slot(a)], last_t, preferred_element_type=jnp.float32)
            x[a] = whole.T.reshape(x.shape[1:])
        near_copy(k).start()

    def send_far(k):
        a = slice(*spans[k])
        near_copy(k).wait_recv()
        for m in range(len(targets)):
            to = place_of(m)
            far_out[m, a] = (x[a, to[0], to[1], core] + near[a, to[0], to[1]]).astype(far_out.dtype)
            far_copy(k, m).start()

    def take(k):
        a = slice(*spans[k])
        total = x[a, z, y, core] + near[a, z, y]
        for m in range(len(targets)):
            far_copy(k, m).wait_recv()
            total = total + far_in[m, a].astype(jnp.float32)
        out_ref[a] = total

    count = len(spans)
    for step in range(count + 2):
        if step == 1:
            for s in range(LAST // t_pair):
                t_far((d - LAST) // t_pair + s).wait_recv()
        if step < count:
            for a in range(*spans[step]):
                for j in range(0, LAST, D_BLOCK):
                    term = integrals(1, a, d - LAST + j, D_BLOCK)
                    for e in range(D_BLOCK):
                        it[:, slot(a, j + e, 1)] = term[e * b:(e + 1) * b]
        if 1 <= step <= count:
            finish(step - 1)
        if step >= 2:
            send_far(step - 2)
    for k in range(count):
        take(k)

    def drain(g, carry):
        for s in range(1, zs):
            z_copy(g, s).wait_send()
        y_copy(g).wait_send()
        core_copy(g).wait_send()
        return carry

    lax.fori_loop(0, slabs, drain, 0)

    def drain_t(i, carry):
        t_far(i).wait_send()
        return carry

    lax.fori_loop(0, xt_send.shape[0], drain_t, 0)
    w_far.wait_send()
    for k in range(len(spans)):
        near_copy(k).wait_send()
        for m in range(len(targets)):
            far_copy(k, m).wait_send()


def fused_call(cols, chol_window, pair_vectors, amplitudes):
    c, widths, q_own = chol_window.shape
    b, d, q = pair_vectors.shape
    n = amplitudes.shape[2]
    zs, ys, cores = routes(cols)
    slabs = 2 * widths
    sends = d // T_PAIR
    rows = widths * b
    n_own = n // cols
    ends = [round(widths * f) for f in SPANS]
    spans = list(zip([0, *ends], [*ends, widths]))
    groups = len(spans)
    dma = pltpu.SemaphoreType.DMA
    hbm = pl.BlockSpec(memory_space=pl.ANY)
    return pl.pallas_call(
        functools.partial(fused_kernel, cols, spans),
        out_shape=jax.ShapeDtypeStruct((widths, n_own, b), jnp.float32),
        in_specs=[hbm, hbm, hbm],
        out_specs=pl.BlockSpec(memory_space=pltpu.VMEM),
        scratch_shapes=[
            pltpu.VMEM((d, b, q), jnp.bfloat16),
            pltpu.VMEM((2, P_ROWS, d, q), jnp.bfloat16),
            pltpu.VMEM((2, widths, zs, ys, cores, q_own, c), jnp.bfloat16),
            pltpu.VMEM((2, d, c, n), jnp.bfloat16),
            pltpu.VMEM((c, d, n), jnp.bfloat16),
            pltpu.VMEM((b, d * c), jnp.bfloat16),
            pltpu.VMEM((rows, D_BLOCK * c), jnp.bfloat16),
            pltpu.VMEM((rows, n), jnp.float32),
            pltpu.VMEM((widths, zs, ys, cores, n_own, b), jnp.float32),
            pltpu.VMEM((widths, zs, ys, n_own, b), jnp.float32),
            pltpu.VMEM((zs * ys - 1, widths, n_own, b), jnp.bfloat16),
            pltpu.VMEM((zs * ys - 1, widths, n_own, b), jnp.bfloat16),
            dma((2,)), dma, dma, dma, dma, dma((sends,)), dma((sends,)),
            dma((slabs, zs - 1)), dma((slabs, zs - 1)),
            dma((slabs,)), dma((slabs,)), dma((slabs,)), dma((slabs,)),
            dma((groups,)), dma((groups,)),
            dma((groups, zs * ys - 1)), dma((groups, zs * ys - 1)),
        ],
        cost_estimate=pl.CostEstimate(
            flops=2 * d * b * 2 * c * widths * (q + n), bytes_accessed=2 * (b * d * q + c * d * n), transcendentals=0),
        compiler_params=pltpu.CompilerParams(collective_id=1, has_side_effects=True, vmem_limit_bytes=60 * 2**20),
    )(chol_window.transpose(1, 2, 0), pair_vectors, amplitudes)


def fits(rows, cols, chol_window, pair_vectors, amplitudes):
    c, widths, q_own = chol_window.shape
    b, d, q = pair_vectors.shape
    n = amplitudes.shape[2]
    held = 2 * (d * b * q + 2 * P_ROWS * d * q + 2 * widths * q * c + 3 * d * c * n + b * d * c + widths * b * D_BLOCK * c)
    held += 16 * widths * b * n
    return (rows == 2 and cols % 4 == 0 and cols > 4 and widths % 8 == 0 and c % 128 == 0 and n % 128 == 0 and q % 128 == 0
            and b % P_ROWS == 0 and b // P_ROWS >= 3 and d % (2 * GROUP) == 0 and LAST <= d // 4 and q_own % GROUP == 0 and n % (cols * GROUP) == 0
            and T_AHEAD + T_EACH * (widths - 1) >= d // T_PAIR
            and held <= 58 * 2**20)


def local(row_count, col_count, chol_window, pair_vectors, amplitudes):
    c, width_a, q_own = chol_window.shape
    b = pair_vectors.shape[0]

    if fits(row_count, col_count, chol_window, pair_vectors, amplitudes):
        return fused_call(col_count, chol_window, pair_vectors, amplitudes)

    w_own = chol_window.transpose(2, 1, 0)
    t_own = amplitudes.transpose(1, 0, 2)
    if row_count == 1:
        blocks = [(w_own, t_own)]
    elif c % 128 == 0:
        blocks = [(w_own, t_own)]
        for shift in range(1, row_count):
            pairs = [(i, (i + shift) % row_count) for i in range(row_count)]
            w_far, t_held = lax.optimization_barrier((lax.ppermute(w_own, "row", pairs), t_own))
            blocks.append((w_far, lax.ppermute(t_held, "row", pairs)))
    else:
        blocks = [(
            lax.all_gather(w_own, "row", axis=2, tiled=True),
            lax.all_gather(t_own, "row", axis=1, tiled=True),
        )]
    p_t = pair_vectors.transpose(1, 0, 2)

    total = None
    for index, (w, t) in enumerate(blocks):
        w = lax.all_gather(w.reshape(q_own, -1), "col", axis=0, tiled=True)
        total = ladder_call(p_t, w, t, total, index == len(blocks) - 1)
    out = scatter_call(total, col_count)
    return out.reshape(out.shape[0], width_a, b).transpose(1, 0, 2)


def solution(mesh):
    return jax.shard_map(
        functools.partial(local, mesh.shape["row"], mesh.shape["col"]),
        mesh=mesh,
        in_specs=(P("row", None, "col"), P("row", "col", None), P("row", "col", None)),
        out_specs=P(None, "col", "row"),
        check_vma=False,
    )
```

```python
import functools

import jax
import jax.numpy as jnp
from jax import lax
from jax.experimental import pallas as pl
from jax.experimental.pallas import tpu as pltpu
from jax.sharding import PartitionSpec as P

MESH = pl.DeviceIdType.MESH
D_BLOCK = 4
P_ROWS = 32
T_PAIR = 2
T_AHEAD = 4
T_EACH = 2
SPANS = (0.25, 0.5, 0.75, 0.875)
LAST = 8


def ladder_kernel(c, last, first, p_ref, w_ref, t_ref, *rest):
    if first:
        out_ref, it, acc = rest
    else:
        prev_ref, out_ref, it, acc = rest
    step = pl.program_id(0)
    d_block, b, q = p_ref.shape
    groups = w_ref.shape[1] // c
    n = t_ref.shape[2]

    @pl.when(step == 0)
    def _():
        acc[...] = jnp.zeros_like(acc) if first else prev_ref[...]

    rows = p_ref[...].reshape(d_block * b, q)
    for a in range(groups):
        term = jnp.dot(rows, w_ref[:, a * c:(a + 1) * c], preferred_element_type=jnp.float32)
        term = term.astype(jnp.bfloat16)
        for d in range(d_block):
            it[a * b:(a + 1) * b, d * c:(d + 1) * c] = term[d * b:(d + 1) * b]
    acc[...] += jnp.dot(it[...], t_ref[...].reshape(d_block * c, n), preferred_element_type=jnp.float32)

    @pl.when(step == pl.num_programs(0) - 1)
    def _():
        out_ref[...] = acc[...].T if last else acc[...]


def ladder_call(p_t, w, t, prev, last):
    d, b, q = p_t.shape
    c, n = t.shape[1], t.shape[2]
    width = w.shape[1]
    rows = width // c * b
    d_block = D_BLOCK if d % D_BLOCK == 0 else 1
    out = (n, rows) if last else (rows, n)
    whole = lambda shape: pl.BlockSpec(shape, lambda i: (0,) * len(shape))
    in_specs = [
        pl.BlockSpec((d_block, b, q), lambda i: (i, 0, 0)),
        whole((q, width)),
        pl.BlockSpec((d_block, c, n), lambda i: (i, 0, 0)),
    ]
    args = [p_t, w, t]
    if prev is not None:
        in_specs.append(whole((rows, n)))
        args.append(prev)
    flops = 2 * d * b * width * (q + n)
    return pl.pallas_call(
        functools.partial(ladder_kernel, c, last, prev is None),
        out_shape=jax.ShapeDtypeStruct(out, jnp.float32),
        grid=(d // d_block,),
        in_specs=in_specs,
        out_specs=whole(out),
        scratch_shapes=[
            pltpu.VMEM((rows, d_block * c), jnp.bfloat16),
            pltpu.VMEM((rows, n), jnp.float32),
        ],
        cost_estimate=pl.CostEstimate(flops=flops, bytes_accessed=2 * (p_t.size + w.size + t.size), transcendentals=0),
        compiler_params=pltpu.CompilerParams(vmem_limit_bytes=60 * 2**20),
    )(*args)


def scatter_kernel(cols, pair, x_ref, out_ref, near, sums, far, near_send, near_recv, far_send, far_recv):
    me = lax.axis_index("col")
    pairs = cols // pair
    core, mine = lax.rem(me, pair), lax.div(me, pair)
    partner = mine * pair + lax.rem(core + 1, pair)

    def place(s):
        return lax.rem(mine + s, pairs) * pair

    barrier = pltpu.get_barrier_semaphore()
    others = [place(s) + core for s in range(1, pairs)] + [partner] * (pair - 1)
    for other in others:
        pl.semaphore_signal(barrier, inc=1, device_id={"col": other}, device_id_type=MESH)
    pl.semaphore_wait(barrier, len(others))

    order = [*range(1, pairs), 0]
    near_copies = {}
    if pair == 2:
        for s in order:
            near_copies[s] = pltpu.make_async_remote_copy(
                src_ref=x_ref.at[place(s) + lax.rem(core + 1, pair)],
                dst_ref=near.at[s],
                send_sem=near_send.at[s],
                recv_sem=near_recv.at[s],
                device_id={"col": partner},
                device_id_type=MESH,
            )
            near_copies[s].start()

    def pair_sum(s):
        own = x_ref[place(s) + core]
        if pair == 1:
            return own
        near_copies[s].wait_recv()
        return own + near[s]

    far_copies = []
    for s in range(1, pairs):
        sums[s - 1] = pair_sum(s).astype(sums.dtype)
        copy = pltpu.make_async_remote_copy(
            src_ref=sums.at[s - 1],
            dst_ref=far.at[s - 1],
            send_sem=far_send.at[s - 1],
            recv_sem=far_recv.at[s - 1],
            device_id={"col": place(s) + core},
            device_id_type=MESH,
        )
        copy.start()
        far_copies.append(copy)
    total = pair_sum(0)
    for s, copy in enumerate(far_copies):
        copy.wait_recv()
        total = total + far[s].astype(jnp.float32)
    out_ref[...] = total
    for copy in far_copies:
        copy.wait_send()
    for copy in near_copies.values():
        copy.wait_send()


def scatter_call(x, cols):
    n, width = x.shape
    piece = (n // cols, width)
    pair = 2 if cols % 2 == 0 else 1
    pairs = cols // pair
    far = max(pairs - 1, 1)
    return pl.pallas_call(
        functools.partial(scatter_kernel, cols, pair),
        out_shape=jax.ShapeDtypeStruct(piece, jnp.float32),
        in_specs=[pl.BlockSpec(memory_space=pltpu.VMEM)],
        out_specs=pl.BlockSpec(memory_space=pltpu.VMEM),
        scratch_shapes=[
            pltpu.VMEM((pairs, *piece), jnp.float32),
            pltpu.VMEM((far, *piece), jnp.bfloat16),
            pltpu.VMEM((far, *piece), jnp.bfloat16),
            pltpu.SemaphoreType.DMA((pairs,)),
            pltpu.SemaphoreType.DMA((pairs,)),
            pltpu.SemaphoreType.DMA((far,)),
            pltpu.SemaphoreType.DMA((far,)),
        ],
        compiler_params=pltpu.CompilerParams(collective_id=0, has_side_effects=True),
    )(x.reshape(cols, *piece))


GROUP = 16


def routes(cols):
    return cols // 4, 2, 2


def fused_kernel(cols, spans, w_in, p_in, t_in, out_ref, pt, p_raw, w, tt, t_raw, it, it_far, acc,
                 x, near, far_out, far_in,
                 p_sem, t_sem, own_sem, xw_send, xw_recv, xt_send, xt_recv,
                 z_send, z_recv, y_send, y_recv, core_send, core_recv,
                 f_send, f_recv, near_send, near_recv, far_send, far_recv):
    d, b, q = pt.shape
    widths = w_in.shape[0]
    c, n = tt.shape[2], tt.shape[3]
    zs, _, _ = routes(cols)
    row, me = lax.axis_index("row"), lax.axis_index("col")
    core, y, z = lax.rem(me, 2), lax.rem(lax.div(me, 2), 2), lax.div(me, 4)
    slabs = 2 * widths
    p_rows = p_raw.shape[1]
    p_parts = b // p_rows
    t_pair = d // xt_send.shape[0]

    def col(z, y, core):
        return {"col": (z * 2 + y) * 2 + core}

    def p_copy(i):
        slot = lax.rem(i, 2)
        return pltpu.make_async_copy(p_in.at[pl.ds(i * p_rows, p_rows)], p_raw.at[slot], p_sem.at[slot])

    t_copy = pltpu.make_async_copy(t_in, t_raw, t_sem)
    own_copy = pltpu.make_async_copy(w_in, w.at[0, :, z, y, core], own_sem)
    own_copy.start()
    t_copy.start()
    p_copy(0).start()
    p_copy(1).start()

    barrier = pltpu.get_barrier_semaphore()
    others = [col(lax.rem(z + s, zs), y, core) for s in range(1, zs)]
    others += [col(lax.rem(z + s, zs), 1 - y, core) for s in range(zs)]
    others += [col(z, y, 1 - core), {"row": 1 - row}]
    for other in others:
        pl.semaphore_signal(barrier, inc=1, device_id=other, device_id_type=MESH)
    pl.semaphore_wait(barrier, len(others))

    def remote(src, dst, send, recv, device):
        return pltpu.make_async_remote_copy(
            src_ref=src, dst_ref=dst, send_sem=send, recv_sem=recv, device_id=device, device_id_type=MESH)

    def place(g):
        return lax.div(g, widths), lax.rem(g, widths)

    def z_copy(g, s):
        h, a = place(g)
        piece = w.at[h, a, z, y, core]
        return remote(piece, piece, z_send.at[g, s - 1], z_recv.at[g, s - 1], col(lax.rem(z + s, zs), y, core))

    def y_copy(g):
        h, a = place(g)
        piece = w.at[h, a, :, y, core]
        return remote(piece, piece, y_send.at[g], y_recv.at[g], col(z, 1 - y, core))

    def core_copy(g):
        h, a = place(g)
        piece = w.at[h, a, :, :, core]
        return remote(piece, piece, core_send.at[g], core_recv.at[g], col(z, y, 1 - core))

    def t_far(i):
        piece = pl.ds(i * t_pair, t_pair)
        return remote(tt.at[0, piece], tt.at[1, piece], xt_send.at[i], xt_recv.at[i], {"row": 1 - row})

    w_far = remote(w_in, w.at[1, :, z, y, core], xw_send, xw_recv, {"row": 1 - row})

    def send_z(g):
        for s in range(1, zs):
            z_copy(g, s).start()

    def send_y(g):
        for s in range(1, zs):
            z_copy(g, s).wait_recv()
        y_copy(g).start()

    def send_core(g):
        y_copy(g).wait_recv()
        core_copy(g).start()

    def first_y(s):
        piece = w.at[0, 0, lax.rem(z - s + zs, zs), y, core]
        return remote(piece, piece, f_send.at[s], f_recv.at[s], col(z, 1 - y, core))

    own_copy.wait()
    send_z(0)
    first_y(0).start()
    w_far.start()
    send_z(1)

    index = lax.broadcasted_iota(jnp.int32, (GROUP * GROUP, GROUP * GROUP), 0)
    source = lax.broadcasted_iota(jnp.int32, (GROUP * GROUP, GROUP * GROUP), 1)
    swap = (lax.rem(index, GROUP) * GROUP + lax.div(index, GROUP) == source).astype(jnp.bfloat16)

    def swapped(block):
        width = block.shape[2]
        moved = jnp.dot(swap, block.reshape(GROUP * GROUP, width), preferred_element_type=jnp.float32)
        return moved.astype(jnp.bfloat16).reshape(GROUP, GROUP, width)

    t_copy.wait()
    for j in range(0, d, GROUP):
        for i in range(0, c, GROUP):
            tt[0, j:j + GROUP, i:i + GROUP] = swapped(t_raw[i:i + GROUP, j:j + GROUP])
        if j == 0:
            for i in range(T_AHEAD):
                t_far(i).start()

    def arrange(i, carry):
        p_copy(i).wait()
        slot = lax.rem(i, 2)
        for r in range(0, p_rows, GROUP):
            for j in range(0, d, GROUP):
                rows = pl.ds(pl.multiple_of(i * p_rows + r, GROUP), GROUP)
                pt[j:j + GROUP, rows] = swapped(p_raw[slot, r:r + GROUP, j:j + GROUP])

        @pl.when(i + 2 < p_parts)
        def _():
            p_copy(i + 2).start()

        return carry

    cut1, cut2 = p_parts // 2 - 1, p_parts - 2
    lax.fori_loop(0, cut1, arrange, 0)
    for s in range(1, zs):
        z_copy(0, s).wait_recv()
        first_y(s).start()
    send_z(2)
    lax.fori_loop(cut1, cut2, arrange, 0)
    for s in range(zs):
        first_y(s).wait_recv()
    core_copy(0).start()
    send_y(1)
    send_z(3)
    lax.fori_loop(cut2, p_parts, arrange, 0)
    send_y(2)
    send_z(4)
    w_far.wait_recv()

    def integrals(h, a, j, block):
        rows = pt[j:j + block].reshape(block * b, q) if isinstance(j, int) else pt[pl.ds(j, block)].reshape(block * b, q)
        term = jnp.dot(rows, w[h, a].reshape(q, c), preferred_element_type=jnp.float32)
        return term.astype(jnp.bfloat16)

    half = d // 2

    def each(first, last, send):
        def body(g, carry):
            send(g)
            return carry

        lax.fori_loop(first + 1, jnp.minimum(last, slabs - 1) + 1, body, 0)

    def held(step):
        return jnp.maximum(2 * step - 1, step + 1)

    def passed(step):
        return jnp.maximum(2 * step + 2, 3)

    def advance(step):
        each(held(step - 1), held(step), send_core)
        each(passed(step - 1), passed(step), send_y)
        each(2 * step + 3, 2 * step + 5, send_z)

    def own_part(a, first, last):
        for j in range(first, last, D_BLOCK):
            term = integrals(0, a, j, D_BLOCK)
            for e in range(D_BLOCK):
                it[:, (j + e) * c:(j + e + 1) * c] = term[e * b:(e + 1) * b]

    def own_end(a):
        acc[pl.ds(a * b, b)] = jnp.dot(it[...], tt[0].reshape(d * c, n), preferred_element_type=jnp.float32)

    core_copy(0).wait_recv()
    own_part(0, 0, half)
    send_core(1)
    send_y(3)
    send_z(5)
    own_part(0, half, d)
    own_end(0)

    def own(a, carry):
        advance(a)
        for i in range(T_EACH):
            i = T_AHEAD + T_EACH * (a - 1) + i

            @pl.when(i < xt_send.shape[0])
            def _():
                t_far(i).start()

        core_copy(a).wait_recv()
        own_part(a, 0, d)
        own_end(a)
        return carry

    lax.fori_loop(1, widths, own, 0)
    for i in range(half // t_pair):
        t_far(i).wait_recv()

    def far(i, carry):
        for e in range(2):
            advance(widths + 2 * i + e)
        for e in range(2):
            core_copy(widths + 2 * i + e).wait_recv()
        for e in range(2):
            for j in range(0, half, D_BLOCK):
                term = integrals(1, 2 * i + e, j, D_BLOCK)
                for k in range(D_BLOCK):
                    at = (e * half + j + k) * c
                    it[:, at:at + c] = term[k * b:(k + 1) * b]
        for e in range(2):
            acc[pl.ds((2 * i + e) * b, b)] += jnp.dot(
                it[:, e * half * c:(e + 1) * half * c], tt[1, :half].reshape(half * c, n),
                preferred_element_type=jnp.float32)
        return carry

    lax.fori_loop(0, widths // 2, far, 0)

    def late(i, carry):
        j = half + i * D_BLOCK
        for a in range(widths):
            term = integrals(1, a, j, D_BLOCK)
            for e in range(D_BLOCK):
                it_far[a * b:(a + 1) * b, e * c:(e + 1) * c] = term[e * b:(e + 1) * b]
        for s in range(D_BLOCK // t_pair):
            t_far(lax.div(j, t_pair) + s).wait_recv()
        acc[...] += jnp.dot(
            it_far[...], tt[1, pl.ds(j, D_BLOCK)].reshape(D_BLOCK * c, n), preferred_element_type=jnp.float32)
        return carry

    lax.fori_loop(0, half // D_BLOCK - LAST // D_BLOCK, late, 0)

    def near_copy(k):
        a = slice(*spans[k])
        return remote(x.at[a, :, :, 1 - core], near.at[a], near_send.at[k], near_recv.at[k], col(z, y, 1 - core))

    targets = [(s, side) for s in range(zs) for side in range(2)][1:]

    def place_of(m):
        s, side = targets[m]
        return lax.rem(z + s, zs), lax.rem(y + side, 2)

    def far_copy(k, m):
        a = slice(*spans[k])
        to = place_of(m)
        return remote(far_out.at[m, a], far_in.at[m, a], far_send.at[k, m], far_recv.at[k, m], col(*to, core))

    def slot(a, e=0, count=LAST):
        first = (a % (d // LAST)) * LAST + e
        return slice(first * c, (first + count) * c)

    def finish(k):
        for a in range(*spans[k]):
            r = slice(a * b, (a + 1) * b)
            last_t = tt[1, d - LAST:].reshape(LAST * c, n)
            whole = acc[r] + jnp.dot(it[:, slot(a)], last_t, preferred_element_type=jnp.float32)
            x[a] = whole.T.reshape(x.shape[1:])
        near_copy(k).start()

    def send_far(k):
        a = slice(*spans[k])
        near_copy(k).wait_recv()
        for m in range(len(targets)):
            to = place_of(m)
            far_out[m, a] = (x[a, to[0], to[1], core] + near[a, to[0], to[1]]).astype(far_out.dtype)
            far_copy(k, m).start()

    def take(k):
        a = slice(*spans[k])
        total = x[a, z, y, core] + near[a, z, y]
        for m in range(len(targets)):
            far_copy(k, m).wait_recv()
            total = total + far_in[m, a].astype(jnp.float32)
        out_ref[a] = total

    count = len(spans)
    for step in range(count + 2):
        if step == 1:
            for s in range(LAST // t_pair):
                t_far((d - LAST) // t_pair + s).wait_recv()
        if step < count:
            for a in range(*spans[step]):
                for j in range(0, LAST, D_BLOCK):
                    term = integrals(1, a, d - LAST + j, D_BLOCK)
                    for e in range(D_BLOCK):
                        it[:, slot(a, j + e, 1)] = term[e * b:(e + 1) * b]
        if 1 <= step <= count:
            finish(step - 1)
        if step >= 2:
            send_far(step - 2)
    def drain(g, carry):
        for s in range(1, zs):
            z_copy(g, s).wait_send()
        core_copy(g).wait_send()
        return carry

    def drain_y(g, carry):
        y_copy(g).wait_send()
        return carry

    lax.fori_loop(1, slabs, drain_y, 0)
    for s in range(zs):
        first_y(s).wait_send()

    lax.fori_loop(0, slabs, drain, 0)

    def drain_t(i, carry):
        t_far(i).wait_send()
        return carry

    lax.fori_loop(0, xt_send.shape[0], drain_t, 0)
    w_far.wait_send()
    for k in range(count):
        take(k)

    for k in range(len(spans)):
        near_copy(k).wait_send()
        for m in range(len(targets)):
            far_copy(k, m).wait_send()


def fused_call(cols, chol_window, pair_vectors, amplitudes):
    c, widths, q_own = chol_window.shape
    b, d, q = pair_vectors.shape
    n = amplitudes.shape[2]
    zs, ys, cores = routes(cols)
    slabs = 2 * widths
    sends = d // T_PAIR
    rows = widths * b
    n_own = n // cols
    ends = [round(widths * f) for f in SPANS]
    spans = list(zip([0, *ends], [*ends, widths]))
    groups = len(spans)
    dma = pltpu.SemaphoreType.DMA
    hbm = pl.BlockSpec(memory_space=pl.ANY)
    return pl.pallas_call(
        functools.partial(fused_kernel, cols, spans),
        out_shape=jax.ShapeDtypeStruct((widths, n_own, b), jnp.float32),
        in_specs=[hbm, hbm, hbm],
        out_specs=pl.BlockSpec(memory_space=pltpu.VMEM),
        scratch_shapes=[
            pltpu.VMEM((d, b, q), jnp.bfloat16),
            pltpu.VMEM((2, P_ROWS, d, q), jnp.bfloat16),
            pltpu.VMEM((2, widths, zs, ys, cores, q_own, c), jnp.bfloat16),
            pltpu.VMEM((2, d, c, n), jnp.bfloat16),
            pltpu.VMEM((c, d, n), jnp.bfloat16),
            pltpu.VMEM((b, d * c), jnp.bfloat16),
            pltpu.VMEM((rows, D_BLOCK * c), jnp.bfloat16),
            pltpu.VMEM((rows, n), jnp.float32),
            pltpu.VMEM((widths, zs, ys, cores, n_own, b), jnp.float32),
            pltpu.VMEM((widths, zs, ys, n_own, b), jnp.float32),
            pltpu.VMEM((zs * ys - 1, widths, n_own, b), jnp.bfloat16),
            pltpu.VMEM((zs * ys - 1, widths, n_own, b), jnp.bfloat16),
            dma((2,)), dma, dma, dma, dma, dma((sends,)), dma((sends,)),
            dma((slabs, zs - 1)), dma((slabs, zs - 1)),
            dma((slabs,)), dma((slabs,)), dma((slabs,)), dma((slabs,)),
            dma((zs,)), dma((zs,)), dma((groups,)), dma((groups,)),
            dma((groups, zs * ys - 1)), dma((groups, zs * ys - 1)),
        ],
        cost_estimate=pl.CostEstimate(
            flops=2 * d * b * 2 * c * widths * (q + n), bytes_accessed=2 * (b * d * q + c * d * n), transcendentals=0),
        compiler_params=pltpu.CompilerParams(collective_id=1, has_side_effects=True, vmem_limit_bytes=60 * 2**20),
    )(chol_window.transpose(1, 2, 0), pair_vectors, amplitudes)


def fits(rows, cols, chol_window, pair_vectors, amplitudes):
    c, widths, q_own = chol_window.shape
    b, d, q = pair_vectors.shape
    n = amplitudes.shape[2]
    held = 2 * (d * b * q + 2 * P_ROWS * d * q + 2 * widths * q * c + 3 * d * c * n + b * d * c + widths * b * D_BLOCK * c)
    held += 16 * widths * b * n
    return (rows == 2 and cols % 4 == 0 and cols > 4 and widths % 8 == 0 and c % 128 == 0 and n % 128 == 0 and q % 128 == 0
            and b % P_ROWS == 0 and b // P_ROWS >= 3 and d % (2 * GROUP) == 0 and LAST <= d // 4 and q_own % GROUP == 0 and n % (cols * GROUP) == 0
            and T_AHEAD + T_EACH * (widths - 1) >= d // T_PAIR
            and held <= 58 * 2**20)


def local(row_count, col_count, chol_window, pair_vectors, amplitudes):
    c, width_a, q_own = chol_window.shape
    b = pair_vectors.shape[0]

    if fits(row_count, col_count, chol_window, pair_vectors, amplitudes):
        return fused_call(col_count, chol_window, pair_vectors, amplitudes)

    w_own = chol_window.transpose(2, 1, 0)
    t_own = amplitudes.transpose(1, 0, 2)
    if row_count == 1:
        blocks = [(w_own, t_own)]
    elif c % 128 == 0:
        blocks = [(w_own, t_own)]
        for shift in range(1, row_count):
            pairs = [(i, (i + shift) % row_count) for i in range(row_count)]
            w_far, t_held = lax.optimization_barrier((lax.ppermute(w_own, "row", pairs), t_own))
            blocks.append((w_far, lax.ppermute(t_held, "row", pairs)))
    else:
        blocks = [(
            lax.all_gather(w_own, "row", axis=2, tiled=True),
            lax.all_gather(t_own, "row", axis=1, tiled=True),
        )]
    p_t = pair_vectors.transpose(1, 0, 2)

    total = None
    for index, (w, t) in enumerate(blocks):
        w = lax.all_gather(w.reshape(q_own, -1), "col", axis=0, tiled=True)
        total = ladder_call(p_t, w, t, total, index == len(blocks) - 1)
    out = scatter_call(total, col_count)
    return out.reshape(out.shape[0], width_a, b).transpose(1, 0, 2)


def solution(mesh):
    return jax.shard_map(
        functools.partial(local, mesh.shape["row"], mesh.shape["col"]),
        mesh=mesh,
        in_specs=(P("row", None, "col"), P("row", "col", None), P("row", "col", None)),
        out_specs=P(None, "col", "row"),
        check_vma=False,
    )
```
